256 devices in a mesh: row: 16 (over y, x), col: 16 (over z, core).
Axes of the slice: x: 4, y: 4, z: 8, core: 2. Of those that a mesh axis runs over, the one named last changes fastest.
Arguments:
- inputs: bfloat16 [512, 8192], P('col', 'row'), may hold values from -6 to 6
- gate_weight: bfloat16 [8192, 28672], P('row', 'col'), may hold values from -0.0625 to 0.0625
- up_weight: bfloat16 [8192, 28672], P('row', 'col'), may hold values from -0.0625 to 0.0625
- down_weight: bfloat16 [28672, 8192], P('col', 'row'), may hold values from -0.03125 to 0.03125
- out_grad: bfloat16 [512, 8192], P('col', 'row'), may hold values from -1.5 to 1.5
Outputs:
- output: bfloat16 [512, 8192], P('col', 'row')
- in_grad: bfloat16 [512, 8192], P('col', 'row')
- gate_grad: bfloat16 [8192, 28672], P('row', 'col')
- up_grad: bfloat16 [8192, 28672], P('row', 'col')
- down_grad: bfloat16 [28672, 8192], P('col', 'row')
The draws below stay inside these ranges and needn't reach their ends.
All inputs are finite; a program needn't handle non-finite values.
Results may differ from the reference program's by a relative error of at most 0.005.
Values may be sent and summed in bfloat16 or wider, within the bound.
No kernel may reach another device: no remote copies, remote signals or barrier semaphores. Data moves between devices by JAX's collectives and lax.ppermute only.
A program may use at most 128 MiB of HBM per device.

```python
import jax
import jax.numpy as jnp
from jax import lax

D = 8192
FF = 28672
TOKENS = 512


def levels(key, dims, shards, low, largest):
    gain, own = 1.0, jax.random.fold_in(key, 6)
    for position, blocks in shards:
        heights = jnp.exp(jax.random.uniform(jax.random.fold_in(own, position), (blocks,), jnp.float32, low / len(shards), largest / len(shards)))
        gain = gain * jnp.repeat(heights, dims[position] // blocks).reshape([-1 if axis == position else 1 for axis in range(len(dims))])
    return gain


def normal_values(stream_key, dims, deviation, reach, pieces=(), held_as=jnp.bfloat16):
    values = deviation * jax.random.normal(stream_key, dims, jnp.float32)
    if pieces:
        values = values * levels(stream_key, dims, pieces, -0.22, 0.18)
    return jnp.clip(values, -reach, reach).astype(held_as)


def setup_inputs(seed: int = 0) -> dict:
    key_list = jax.random.split(jax.random.key(seed), 6)
    inputs = normal_values(key_list[0], (TOKENS, D), 1.0, 6.0, ((0, 16), (1, 16)))
    gate_weight = normal_values(key_list[1], (D, FF), D ** -0.5, 0.0625, ((0, 16), (1, 16)))
    up_weight = normal_values(key_list[2], (D, FF), D ** -0.5, 0.0625, ((0, 16), (1, 16)))
    down_weight = normal_values(key_list[3], (FF, D), FF ** -0.5, 0.03125, ((0, 16), (1, 16)))
    out_grad = normal_values(key_list[4], (TOKENS, D), 0.25, 1.5, ((0, 16), (1, 16)))
    return {"inputs": inputs, "gate_weight": gate_weight, "up_weight": up_weight, "down_weight": down_weight, "out_grad": out_grad}


def contract_first(left, right):
    return lax.dot_general(left, right, (((0,), (0,)), ((), ())), preferred_element_type=jnp.float32)


def contract_last(left, right):
    return lax.dot_general(left, right, (((1,), (1,)), ((), ())), preferred_element_type=jnp.float32)


def reference(inputs, gate_weight, up_weight, down_weight, out_grad):
    gate_value = jnp.dot(inputs, gate_weight, preferred_element_type=jnp.float32)
    up_value = jnp.dot(inputs, up_weight, preferred_element_type=jnp.float32)
    sigmoid_gate = jax.nn.sigmoid(gate_value)
    hidden = (gate_value * sigmoid_gate * up_value).astype(jnp.bfloat16)
    output = jnp.dot(hidden, down_weight, preferred_element_type=jnp.float32).astype(jnp.bfloat16)
    hidden_grad = contract_last(out_grad, down_weight)
    slope = sigmoid_gate * (1.0 + gate_value * (1.0 - sigmoid_gate))
    gate_part = (hidden_grad * up_value * slope).astype(jnp.bfloat16)
    up_part = (hidden_grad * gate_value * sigmoid_gate).astype(jnp.bfloat16)
    in_grad = (contract_last(gate_part, gate_weight) + contract_last(up_part, up_weight)).astype(jnp.bfloat16)
    gate_grad = contract_first(inputs, gate_part).astype(jnp.bfloat16)
    up_grad = contract_first(inputs, up_part).astype(jnp.bfloat16)
    down_grad = contract_first(hidden, out_grad).astype(jnp.bfloat16)
    return output, in_grad, gate_grad, up_grad, down_grad
```

```python
import functools

import jax
import jax.numpy as jnp
from jax import lax
from jax.experimental import pallas as pl
from jax.experimental.pallas import tpu as pltpu
from jax.sharding import PartitionSpec as P


BF16, F32 = jnp.bfloat16, jnp.float32
SIDE = 4
DEEP = 8
BLOCKS = 16
VMEM_LIMIT = 56 * 1024 * 1024


def contract(left, right, left_dim, right_dim):
    return lax.dot_general(
        left, right, (((left_dim,), (right_dim,)), ((), ())), preferred_element_type=F32
    )


def row_shift(dy, dx):
    return [
        (SIDE * y + x, SIDE * ((y + dy) % SIDE) + (x + dx) % SIDE)
        for y in range(SIDE)
        for x in range(SIDE)
    ]


def partner():
    return [(c, c ^ 1) for c in range(2 * DEEP)]


def call(kernel, outs, n_scalar, scratch=(), **kwargs):
    vmem = pl.BlockSpec(memory_space=pltpu.VMEM)
    smem = pl.BlockSpec(memory_space=pltpu.SMEM)

    def run(*args):
        specs = [smem] * n_scalar + [vmem] * (len(args) - n_scalar)
        return pl.pallas_call(
            kernel,
            out_shape=[jax.ShapeDtypeStruct(s, d) for s, d in outs],
            in_specs=specs,
            out_specs=[vmem] * len(outs),
            scratch_shapes=scratch,
            compiler_params=pltpu.CompilerParams(vmem_limit_bytes=VMEM_LIMIT),
            **kwargs,
        )(*args)

    return run


def partial_kernel(order, x, og, gw, uw, dw, keep, send1, send2, send3, xs, gs):
    rows = x.shape[0] // BLOCKS
    for s in range(BLOCKS):
        at = pl.ds(pl.multiple_of(order[s] * rows, rows), rows)
        xs[s * rows : (s + 1) * rows] = x[at, :]
        gs[s * rows : (s + 1) * rows] = og[at, :]
    group = SIDE * rows
    for n, (left, weight, dim) in enumerate(((xs, gw, 0), (xs, uw, 0), (gs, dw, 1))):
        value = contract(left[...], weight[...], 1, dim)
        keep[n] = value[:group]
        for k, send in enumerate((send1, send2, send3)):
            send[n] = value[(k + 1) * group : (k + 2) * group].astype(BF16)


def first_sum_kernel(keep, got1, got2, got3, own, send1, send2, send3):
    rows = own.shape[1]
    for k, out in enumerate((own, send1, send2, send3)):
        at = slice(k * rows, (k + 1) * rows)
        total = keep[:, at, :]
        for got in (got1, got2, got3):
            total = total + got[:, at, :].astype(F32)
        out[...] = total.astype(out.dtype)


def gating_kernel(own, got1, got2, got3, out):
    gate, up, grad = (
        own[n] + got1[n].astype(F32) + got2[n].astype(F32) + got3[n].astype(F32)
        for n in range(3)
    )
    sig = jax.nn.sigmoid(gate)
    out[0] = (gate * sig * up).astype(BF16)
    out[1] = (grad * up * (sig * (1.0 + gate * (1.0 - sig)))).astype(BF16)
    out[2] = (grad * gate * sig).astype(BF16)


def rows_of(piece, n):
    return piece[:, n].reshape(-1, piece.shape[-1])


def product_kernel(core, order_a, order_b, *refs):
    pieces_a, pieces_b = refs[:4], refs[4:8]
    gw, uw, dw, mine, theirs, out_sum, in_sum = refs[8:]
    rows = pieces_a[0].shape[2]
    half = pieces_a[0].shape[3]
    for lo, order, pieces in ((0, order_a, pieces_a), (half, order_b, pieces_b)):
        cols = slice(lo, lo + half)
        for k, piece in enumerate(pieces):
            hidden, gate, up = (rows_of(piece, n) for n in range(3))
            output = contract(hidden, dw[cols, :], 1, 0)
            grad = contract(gate, gw[:, cols], 1, 1) + contract(up, uw[:, cols], 1, 1)
            for s in range(SIDE):
                at = pl.ds(pl.multiple_of(order[k * SIDE + s] * rows, rows), rows)
                block = slice(s * rows, (s + 1) * rows)
                if lo:
                    out_sum[at, :] += output[block]
                    in_sum[at, :] += grad[block]
                else:
                    out_sum[at, :] = output[block]
                    in_sum[at, :] = grad[block]

    @pl.when(core[0] == 0)
    def _():
        mine[...] = out_sum[...]
        theirs[...] = in_sum[...]

    @pl.when(core[0] == 1)
    def _():
        mine[...] = in_sum[...]
        theirs[...] = out_sum[...]


def weight_grads_kernel(order_a, order_b, x, og, *refs):
    pieces_a, pieces_b = refs[:4], refs[4:8]
    gate_grad, up_grad, down_grad, xs, gs, stack = refs[8:]
    rows = pieces_a[0].shape[2]
    half = pieces_a[0].shape[3]
    group = SIDE * rows
    for lo, order, pieces in ((0, order_a, pieces_a), (half, order_b, pieces_b)):
        for s in range(BLOCKS):
            at = pl.ds(pl.multiple_of(order[s] * rows, rows), rows)
            xs[s * rows : (s + 1) * rows] = x[at, :]
            gs[s * rows : (s + 1) * rows] = og[at, :]
        for n in range(3):
            for k, piece in enumerate(pieces):
                stack[n, k * group : (k + 1) * group] = rows_of(piece, n)
        cols = slice(lo, lo + half)
        gate_grad[:, cols] = contract(xs[...], stack[1], 0, 0).astype(BF16)
        up_grad[:, cols] = contract(xs[...], stack[2], 0, 0).astype(BF16)
        down_grad[cols, :] = contract(stack[0], gs[...], 0, 0).astype(BF16)


def reduce_half(parts, major, minor, names):
    keep, *sends = parts
    _, group, half = keep.shape
    rows = group // SIDE
    got = [lax.ppermute(s, "row", major(k + 1)) for k, s in enumerate(sends)]
    own, *sends = call(
        first_sum_kernel,
        [((3, rows, half), F32)] + [((3, rows, half), BF16)] * 3,
        0,
        name=names + "_first",
    )(keep, *got)
    got = [lax.ppermute(s, "row", minor(k + 1)) for k, s in enumerate(sends)]
    (shard,) = call(gating_kernel, [((3, rows, half), BF16)], 0, name=names + "_gating")(own, *got)
    return shard


def gather_half(shard, major, minor):
    got = [lax.ppermute(shard, "row", minor(-k)) for k in range(1, SIDE)]
    own = jnp.stack([shard, *got])
    return [own] + [lax.ppermute(own, "row", major(-k)) for k in range(1, SIDE)]


def along_x(k):
    return row_shift(0, k)


def along_y(k):
    return row_shift(k, 0)


def on_device(inputs, gate_weight, up_weight, down_weight, out_grad):
    deep, width = gate_weight.shape
    half = width // 2
    row, col = lax.axis_index("row"), lax.axis_index("col")
    y, x = row // SIDE, row % SIDE
    slot = jnp.arange(BLOCKS, dtype=jnp.int32)
    outer, inner = slot // SIDE, slot % SIDE
    order_a = ((y + inner) % SIDE) * SIDE + (x + outer) % SIDE
    order_b = ((y + outer) % SIDE) * SIDE + (x + inner) % SIDE
    core = (col % 2).reshape(1)

    all_inputs = lax.all_gather(inputs, "col", axis=0, tiled=True)
    all_grads = lax.all_gather(out_grad, "col", axis=0, tiled=True)
    tokens = all_inputs.shape[0]
    rows = tokens // BLOCKS
    group = SIDE * rows

    def partials(order, h):
        vmem = pltpu.VMEM
        return pl.pallas_call(
            partial_kernel,
            name=f"partial_{h}",
            out_shape=[jax.ShapeDtypeStruct((3, group, half), F32)]
            + [jax.ShapeDtypeStruct((3, group, half), BF16)] * 3,
            grid=(1,),
            in_specs=[
                pl.BlockSpec(memory_space=pltpu.SMEM),
                pl.BlockSpec((tokens, deep), lambda i: (0, 0)),
                pl.BlockSpec((tokens, deep), lambda i: (0, 0)),
                pl.BlockSpec((deep, half), lambda i: (0, h)),
                pl.BlockSpec((deep, half), lambda i: (0, h)),
                pl.BlockSpec((half, deep), lambda i: (h, 0)),
            ],
            out_specs=[pl.BlockSpec((3, group, half), lambda i: (0, 0, 0))] * 4,
            scratch_shapes=[vmem((tokens, deep), BF16)] * 2,
            compiler_params=pltpu.CompilerParams(vmem_limit_bytes=VMEM_LIMIT),
        )(order, all_inputs, all_grads, gate_weight, up_weight, down_weight)

    shard_a = reduce_half(partials(order_a, 0), along_x, along_y, "a")
    shard_b = reduce_half(partials(order_b, 1), along_y, along_x, "b")
    pieces_a = gather_half(shard_a, along_x, along_y)
    pieces_b = gather_half(shard_b, along_y, along_x)

    mine, theirs = call(
        product_kernel,
        [((tokens, deep), F32)] * 2,
        3,
        scratch=[pltpu.VMEM((tokens, deep), F32)] * 2,
        name="product",
    )(core, order_a, order_b, *pieces_a, *pieces_b, gate_weight, up_weight, down_weight)
    total = mine + lax.ppermute(theirs, "col", partner())
    same_core = [[2 * z + c for z in range(DEEP)] for c in range(2)]
    got = lax.all_to_all(
        total.astype(BF16), "col", 0, 0, axis_index_groups=same_core, tiled=True
    )
    chip = jnp.sum(got.reshape(DEEP, tokens // DEEP, deep).astype(F32), axis=0).astype(BF16)
    low, high = chip[:rows], chip[rows:]
    first = core[0] == 0
    stay, go = jnp.where(first, low, high), jnp.where(first, high, low)
    come = lax.ppermute(go, "col", partner())
    output, in_grad = jnp.where(first, stay, come), jnp.where(first, come, stay)

    gate_grad, up_grad, down_grad = call(
        weight_grads_kernel,
        [((deep, width), BF16)] * 2 + [((width, deep), BF16)],
        2,
        scratch=[pltpu.VMEM((tokens, deep), BF16)] * 2 + [pltpu.VMEM((3, tokens, half), BF16)],
        name="weight_grads",
    )(order_a, order_b, all_inputs, all_grads, *pieces_a, *pieces_b)
    return (output, in_grad, gate_grad, up_grad, down_grad)


def solution(mesh):
    in_specs = (P("col", "row"), P("row", "col"), P("row", "col"), P("col", "row"), P("col", "row"))
    out_specs = (
        P("col", "row"),
        P("col", "row"),
        P("row", "col"),
        P("row", "col"),
        P("col", "row"),
    )
    return jax.shard_map(
        on_device, mesh=mesh, in_specs=in_specs, out_specs=out_specs, check_vma=False
    )
```

```python
import functools

import jax
import jax.numpy as jnp
from jax import lax
from jax.experimental import pallas as pl
from jax.experimental.pallas import tpu as pltpu
from jax.sharding import PartitionSpec as P


BF16, F32 = jnp.bfloat16, jnp.float32
SIDE = 4
DEEP = 8
BLOCKS = 16
VMEM_LIMIT = 56 * 1024 * 1024


def contract(left, right, left_dim, right_dim):
    return lax.dot_general(
        left, right, (((left_dim,), (right_dim,)), ((), ())), preferred_element_type=F32
    )


def shift(k, along):
    pairs = []
    for y in range(SIDE):
        for x in range(SIDE):
            for c in range(2 * DEEP):
                dy, dx = along if c % 2 == 0 else along[::-1]
                row = (y + k * dy) % SIDE * SIDE + (x + k * dx) % SIDE
                pairs.append(((y * SIDE + x) * 2 * DEEP + c, row * 2 * DEEP + c))
    return pairs


MAJOR, MINOR = (0, 1), (1, 0)


def partner():
    return [(c, c ^ 1) for c in range(2 * DEEP)]


def call(kernel, outs, n_scalar, args, scratch=()):
    vmem = pl.BlockSpec(memory_space=pltpu.VMEM)
    smem = pl.BlockSpec(memory_space=pltpu.SMEM)
    return pl.pallas_call(
        kernel,
        out_shape=[jax.ShapeDtypeStruct(s, d) for s, d in outs],
        in_specs=[smem] * n_scalar + [vmem] * (len(args) - n_scalar),
        out_specs=[vmem] * len(outs),
        scratch_shapes=scratch,
        compiler_params=pltpu.CompilerParams(vmem_limit_bytes=VMEM_LIMIT),
    )(*args)


def take_blocks(order, source, target):
    rows = source.shape[0] // BLOCKS
    for s in range(BLOCKS):
        at = pl.ds(pl.multiple_of(order[s] * rows, rows), rows)
        target[s * rows : (s + 1) * rows] = source[at, :]


def partial_kernel(dim, order, left, *refs):
    *weights, keep, send1, send2, send3, mine = refs
    take_blocks(order, left, mine)
    group = keep.shape[1]
    for n, weight in enumerate(weights):
        value = contract(mine[...], weight[...], 1, dim)
        keep[n] = value[:group]
        for k, send in enumerate((send1, send2, send3)):
            send[n] = value[(k + 1) * group : (k + 2) * group].astype(BF16)


def first_sum_kernel(keep_gu, keep_h, *refs):
    got_gu, got_h, outs = refs[:3], refs[3:6], refs[6:]
    rows = outs[0].shape[1]
    for k, out in enumerate(outs):
        at = slice(k * rows, (k + 1) * rows)
        for keep, gots, lo in ((keep_gu, got_gu, 0), (keep_h, got_h, 2)):
            total = keep[:, at, :]
            for got in gots:
                total = total + got[:, at, :].astype(F32)
            out[lo : lo + keep.shape[0]] = total.astype(out.dtype)


def gating_kernel(own, got1, got2, got3, out):
    gate, up, grad = (
        own[n] + got1[n].astype(F32) + got2[n].astype(F32) + got3[n].astype(F32)
        for n in range(3)
    )
    sig = jax.nn.sigmoid(gate)
    out[0] = (gate * sig * up).astype(BF16)
    out[1] = (grad * up * (sig * (1.0 + gate * (1.0 - sig)))).astype(BF16)
    out[2] = (grad * gate * sig).astype(BF16)


def join_kernel(*refs):
    blocks, outs = refs[: SIDE - 1], refs[SIDE - 1 :]
    rows = blocks[0].shape[1]
    for k, block in enumerate(blocks):
        at = slice(k * rows, (k + 1) * rows)
        lo = 0
        for out in outs:
            n = out.shape[0]
            out[:, at, :] = block[lo : lo + n]
            lo += n


def stack_rows(shards, n, rests, m, target):
    rows, more = shards[0].shape[1], rests[0].shape[1]
    for k, (shard, rest) in enumerate(zip(shards, rests)):
        at = k * (rows + more)
        target[at : at + rows] = shard[n]
        target[at + rows : at + rows + more] = rest[m]


def product_kernel(dim, first, place, *refs):
    shards, rests, weights = refs[:SIDE], refs[SIDE : 2 * SIDE], refs[2 * SIDE : -4]
    mine, theirs, total, stack = refs[-4:]
    tokens = stack.shape[0]
    rows = tokens // BLOCKS
    value = None
    for n, weight in enumerate(weights):
        stack_rows(shards, first + n, rests, n, stack)
        term = contract(stack[...], weight[...], 1, dim)
        value = term if value is None else value + term
    for s in range(BLOCKS):
        at = pl.ds(pl.multiple_of(place[s] * rows, rows), rows)
        total[at, :] = value[s * rows : (s + 1) * rows]
    mine[...] = total[: tokens // 2]
    theirs[...] = total[tokens // 2 :]


def down_grad_kernel(order, og, *refs):
    shards, rests = refs[:SIDE], refs[SIDE : 2 * SIDE]
    down_grad, mine, stack = refs[2 * SIDE :]
    take_blocks(order, og, mine)
    stack_rows(shards, 0, rests, 0, stack)
    down_grad[...] = contract(stack[...], mine[...], 0, 0).astype(BF16)


def weight_grads_kernel(order, x, *refs):
    shards, rests = refs[:SIDE], refs[SIDE : 2 * SIDE]
    gate_grad, up_grad, mine, stack = refs[2 * SIDE :]
    take_blocks(order, x, mine)
    for n, grad in enumerate((gate_grad, up_grad)):
        stack_rows(shards, 1 + n, rests, n, stack)
        grad[...] = contract(mine[...], stack[...], 0, 0).astype(BF16)


def send(value, k, along):
    return lax.ppermute(value, ("row", "col"), shift(k, along))


def spread(values, along):
    return [send(v, k + 1, along) for k, v in enumerate(values)]


def collect(value, along):
    return [value] + [send(value, -k, along) for k in range(1, SIDE)]


def z_reduce(mine, theirs, wire, same_core):
    total = (mine + lax.ppermute(theirs, "col", partner())).astype(wire)
    got = lax.all_to_all(total, "col", 0, 0, axis_index_groups=same_core, tiled=True)
    return jnp.sum(got.reshape(DEEP, -1, got.shape[1]).astype(F32), axis=0).astype(BF16)


def on_device(inputs, gate_weight, up_weight, down_weight, out_grad):
    deep, width = gate_weight.shape
    row, col = lax.axis_index("row"), lax.axis_index("col")
    y, x, core = row // SIDE, row % SIDE, col % 2
    slot = jnp.arange(BLOCKS, dtype=jnp.int32)
    outer, inner = slot // SIDE, slot % SIDE
    dy, dx = jnp.where(core == 0, inner, outer), jnp.where(core == 0, outer, inner)
    order = (y + dy) % SIDE * SIDE + (x + dx) % SIDE
    place = (order + core) % 2 * DEEP + order // 2
    same_core = [[2 * z + c for z in range(DEEP)] for c in range(2)]

    all_inputs = lax.all_gather(inputs, "col", axis=0, tiled=True)
    tokens = all_inputs.shape[0]
    rows = tokens // BLOCKS
    group = SIDE * rows

    def partials(left, weights, dim):
        n = len(weights)
        return call(
            functools.partial(partial_kernel, dim),
            [((n, group, width), F32)] + [((n, group, width), BF16)] * 3,
            1,
            (order, left, *weights),
            [pltpu.VMEM((tokens, deep), BF16)],
        )

    def product(pieces, weights, dim, first):
        return call(
            functools.partial(product_kernel, dim, first),
            [((tokens // 2, deep), F32)] * 2,
            1,
            (place, *pieces, *weights),
            [pltpu.VMEM((tokens, deep), F32), pltpu.VMEM((tokens, width), BF16)],
        )

    keep_gu, *sends = partials(all_inputs, (gate_weight, up_weight), 0)
    got_gu = spread(sends, MAJOR)
    out_grad, keep_gu = lax.optimization_barrier((out_grad, keep_gu))
    all_grads = lax.all_gather(out_grad, "col", axis=0, tiled=True)
    keep_h, *sends = partials(all_grads, (down_weight,), 1)
    got_h = spread(sends, MAJOR)
    own, *sends = call(
        first_sum_kernel,
        [((3, rows, width), F32)] + [((3, rows, width), BF16)] * 3,
        0,
        (keep_gu, keep_h, *got_gu, *got_h),
    )
    (shard,) = call(
        gating_kernel, [((3, rows, width), BF16)], 0, (own, *spread(sends, MINOR))
    )
    blocks = collect(shard, MINOR)[1:]
    shards = collect(shard, MAJOR)
    more = (SIDE - 1) * rows
    hidden, parts = call(
        join_kernel, [((1, more, width), BF16), ((2, more, width), BF16)], 0, blocks
    )
    hiddens = shards + collect(hidden, MAJOR)
    grads = shards + collect(parts, MAJOR)

    scratch = [pltpu.VMEM((tokens, deep), BF16), pltpu.VMEM((tokens, width), BF16)]
    sums = product(hiddens, (down_weight,), 0, 0)
    output = z_reduce(*sums, BF16, same_core)
    (down_grad,) = call(
        down_grad_kernel, [((width, deep), BF16)], 1,
        (order, all_grads, *hiddens), scratch,
    )
    sums = product(grads, (gate_weight, up_weight), 1, 1)
    in_grad = z_reduce(*sums, BF16, same_core)
    gate_grad, up_grad = call(
        weight_grads_kernel, [((deep, width), BF16)] * 2, 1,
        (order, all_inputs, *grads), scratch,
    )
    return (output, in_grad, gate_grad, up_grad, down_grad)


def solution(mesh):
    in_specs = (P("col", "row"), P("row", "col"), P("row", "col"), P("col", "row"), P("col", "row"))
    out_specs = (
        P("col", "row"),
        P("col", "row"),
        P("row", "col"),
        P("row", "col"),
        P("col", "row"),
    )
    return jax.shard_map(
        on_device, mesh=mesh, in_specs=in_specs, out_specs=out_specs, check_vma=False
    )
```

```python
import functools

import jax
import jax.numpy as jnp
from jax import lax
from jax.experimental import pallas as pl
from jax.experimental.pallas import tpu as pltpu
from jax.sharding import PartitionSpec as P


BF16, F32 = jnp.bfloat16, jnp.float32
SIDE = 4
DEEP = 8
BLOCKS = 16
VMEM_LIMIT = 56 * 1024 * 1024


def contract(left, right, left_dim, right_dim):
    return lax.dot_general(
        left, right, (((left_dim,), (right_dim,)), ((), ())), preferred_element_type=F32
    )


def shift(k, along):
    pairs = []
    for y in range(SIDE):
        for x in range(SIDE):
            for c in range(2 * DEEP):
                dy, dx = along if c % 2 == 0 else along[::-1]
                row = (y + k * dy) % SIDE * SIDE + (x + k * dx) % SIDE
                pairs.append(((y * SIDE + x) * 2 * DEEP + c, row * 2 * DEEP + c))
    return pairs


MAJOR, MINOR = (0, 1), (1, 0)


def partner():
    return [(c, c ^ 1) for c in range(2 * DEEP)]


def call(kernel, outs, n_scalar, args, scratch=(), blocks=None, steps=1):
    arrays = [(a.shape, a.dtype) for a in args[n_scalar:]] + list(outs)
    blocks = blocks or [None] * len(arrays)

    def spec(shape, cut):
        size = [d // steps if n == cut else d for n, d in enumerate(shape)]
        return pl.BlockSpec(tuple(size), lambda i: tuple(i if n == cut else 0 for n in range(len(shape))))

    specs = [spec(shape, cut) for (shape, _), cut in zip(arrays, blocks)]
    n_in = len(args) - n_scalar
    return pl.pallas_call(
        kernel,
        grid=(steps,),
        out_shape=[jax.ShapeDtypeStruct(s, d) for s, d in outs],
        in_specs=[pl.BlockSpec(memory_space=pltpu.SMEM)] * n_scalar + specs[:n_in],
        out_specs=specs[n_in:],
        scratch_shapes=scratch,
        compiler_params=pltpu.CompilerParams(vmem_limit_bytes=VMEM_LIMIT),
    )(*args)


def take_blocks(order, source, target):
    rows = source.shape[0] // BLOCKS
    for s in range(BLOCKS):
        at = pl.ds(pl.multiple_of(order[s] * rows, rows), rows)
        target[s * rows : (s + 1) * rows] = source[at, :]


def partial_kernel(dim, order, left, *refs):
    *weights, keep, send1, send2, send3, mine = refs

    @pl.when(pl.program_id(0) == 0)
    def _():
        take_blocks(order, left, mine)

    group = keep.shape[1]
    for n, weight in enumerate(weights):
        value = contract(mine[...], weight[...], 1, dim)
        keep[n] = value[:group]
        for k, send in enumerate((send1, send2, send3)):
            send[n] = value[(k + 1) * group : (k + 2) * group].astype(BF16)


def first_sum_kernel(keep, got1, got2, got3, *outs):
    rows = outs[0].shape[1]
    for k, out in enumerate(outs):
        at = slice(k * rows, (k + 1) * rows)
        total = keep[:, at, :]
        for got in (got1, got2, got3):
            total = total + got[:, at, :].astype(F32)
        out[...] = total.astype(out.dtype)


def last_sum(n, own, *gots):
    return own[n] + sum(got[n].astype(F32) for got in gots)


def hidden_kernel(*refs):
    sums, (hidden, factors) = refs[:SIDE], refs[SIDE:]
    gate, up = last_sum(0, *sums), last_sum(1, *sums)
    sig = jax.nn.sigmoid(gate)
    hidden[0] = (gate * sig * up).astype(BF16)
    factors[0] = up * (sig * (1.0 + gate * (1.0 - sig)))
    factors[1] = gate * sig


def parts_kernel(factors, *refs):
    sums, (parts,) = refs[:SIDE], refs[SIDE:]
    grad = last_sum(0, *sums)
    for n in range(2):
        parts[n] = (grad * factors[n]).astype(BF16)


def join_kernel(*refs):
    blocks, (out,) = refs[:SIDE], refs[SIDE:]
    rows = blocks[0].shape[1]
    for k, block in enumerate(blocks):
        out[:, k * rows : (k + 1) * rows, :] = block[...]


def stack_rows(pieces, n, target):
    rows = pieces[0].shape[1]
    for k, piece in enumerate(pieces):
        target[k * rows : (k + 1) * rows] = piece[n]


def product_kernel(dim, place, *refs):
    pieces, weights = refs[:SIDE], refs[SIDE:-4]
    mine, theirs, total, stack = refs[-4:]
    tokens = stack.shape[0]
    rows = tokens // BLOCKS
    step = pl.program_id(0)
    value = None
    for n, weight in enumerate(weights):
        stack_rows(pieces, n, stack)
        term = contract(stack[...], weight[...], 1, dim)
        value = term if value is None else value + term

    @pl.when(step == 0)
    def _():
        total[...] = value

    @pl.when(step == 1)
    def _():
        for s in range(BLOCKS):
            to = place[s]
            done = total[s * rows : (s + 1) * rows] + value[s * rows : (s + 1) * rows]

            @pl.when(to < DEEP)
            def _():
                mine[pl.ds(pl.multiple_of(to * rows, rows), rows), :] = done

            @pl.when(to >= DEEP)
            def _():
                theirs[pl.ds(pl.multiple_of((to - DEEP) * rows, rows), rows), :] = done


def down_grad_kernel(order, og, *refs):
    pieces, (down_grad, mine, stack) = refs[:SIDE], refs[SIDE:]
    take_blocks(order, og, mine)
    stack_rows(pieces, 0, stack)
    down_grad[...] = contract(stack[...], mine[...], 0, 0).astype(BF16)


def weight_grads_kernel(order, x, *refs):
    pieces, (gate_grad, up_grad, mine, stack) = refs[:SIDE], refs[SIDE:]
    take_blocks(order, x, mine)
    for n, grad in enumerate((gate_grad, up_grad)):
        stack_rows(pieces, n, stack)
        grad[...] = contract(mine[...], stack[...], 0, 0).astype(BF16)


def send(value, k, along):
    return lax.ppermute(value, ("row", "col"), shift(k, along))


def spread(values, along):
    return [send(v, k + 1, along) for k, v in enumerate(values)]


def collect(value, along):
    return [value] + [send(value, -k, along) for k in range(1, SIDE)]


def z_reduce(mine, theirs, wire, same_core):
    total = (mine + lax.ppermute(theirs, "col", partner())).astype(wire)
    got = lax.all_to_all(total, "col", 0, 0, axis_index_groups=same_core, tiled=True)
    return jnp.sum(got.reshape(DEEP, -1, got.shape[1]).astype(F32), axis=0).astype(BF16)


def on_device(inputs, gate_weight, up_weight, down_weight, out_grad):
    deep, width = gate_weight.shape
    row, col = lax.axis_index("row"), lax.axis_index("col")
    y, x, core = row // SIDE, row % SIDE, col % 2
    slot = jnp.arange(BLOCKS, dtype=jnp.int32)
    outer, inner = slot // SIDE, slot % SIDE
    dy, dx = jnp.where(core == 0, inner, outer), jnp.where(core == 0, outer, inner)
    order = (y + dy) % SIDE * SIDE + (x + dx) % SIDE
    place = (order + core) % 2 * DEEP + order // 2
    same_core = [[2 * z + c for z in range(DEEP)] for c in range(2)]

    all_inputs = lax.all_gather(inputs, "col", axis=0, tiled=True)
    tokens = all_inputs.shape[0]
    rows = tokens // BLOCKS
    group = SIDE * rows

    def partials(left, weights, dim):
        n = len(weights)
        return call(
            functools.partial(partial_kernel, dim),
            [((n, group, width), F32)] + [((n, group, width), BF16)] * 3,
            1,
            (order, left, *weights),
            [pltpu.VMEM((tokens, deep), BF16)],
            [None] + [1 - dim] * n + [2] * 4,
            2,
        )

    def product(pieces, weights, dim):
        return call(
            functools.partial(product_kernel, dim),
            [((tokens // 2, deep), F32)] * 2,
            1,
            (place, *pieces, *weights),
            [pltpu.VMEM((tokens, deep), F32), pltpu.VMEM((tokens, width // 2), BF16)],
            [2] * 4 + [dim] * len(weights) + [None] * 2,
            2,
        )

    keep_gu, *sends = partials(all_inputs, (gate_weight, up_weight), 0)
    got_gu = spread(sends, MAJOR)
    out_grad, keep_gu = lax.optimization_barrier((out_grad, keep_gu))
    all_grads = lax.all_gather(out_grad, "col", axis=0, tiled=True)
    keep_h, *sends = partials(all_grads, (down_weight,), 1)
    got_h = spread(sends, MAJOR)

    def first_sum(keep, got):
        n = keep.shape[0]
        return call(
            first_sum_kernel,
            [((n, rows, width), F32)] + [((n, rows, width), BF16)] * 3,
            0,
            (keep, *got),
            blocks=[2] * 8,
            steps=2,
        )

    def join(blocks):
        n = blocks[0].shape[0]
        (out,) = call(join_kernel, [((n, group, width), BF16)], 0, blocks, blocks=[2] * 5, steps=2)
        return out

    own_gu, *sends = first_sum(keep_gu, got_gu)
    got_gu = spread(sends, MINOR)
    own_h, *sends = first_sum(keep_h, got_h)
    got_h = spread(sends, MINOR)
    hidden, factors = call(
        hidden_kernel,
        [((1, rows, width), BF16), ((2, rows, width), F32)],
        0,
        (own_gu, *got_gu),
        blocks=[2] * 6,
        steps=2,
    )
    blocks_hidden = collect(hidden, MINOR)
    (parts,) = call(
        parts_kernel,
        [((2, rows, width), BF16)],
        0,
        (factors, own_h, *got_h),
        blocks=[2] * 6,
        steps=2,
    )
    blocks_parts = collect(parts, MINOR)
    hiddens = collect(join(blocks_hidden), MAJOR)
    grads = collect(join(blocks_parts), MAJOR)

    scratch = [pltpu.VMEM((tokens, deep), BF16), pltpu.VMEM((tokens, width), BF16)]
    sums = product(hiddens, (down_weight,), 0)
    output = z_reduce(*sums, BF16, same_core)
    (down_grad,) = call(
        down_grad_kernel, [((width, deep), BF16)], 1,
        (order, all_grads, *hiddens), scratch,
    )
    sums = product(grads, (gate_weight, up_weight), 1)
    in_grad = z_reduce(*sums, BF16, same_core)
    gate_grad, up_grad = call(
        weight_grads_kernel, [((deep, width), BF16)] * 2, 1,
        (order, all_inputs, *grads), scratch,
    )
    return (output, in_grad, gate_grad, up_grad, down_grad)


def solution(mesh):
    in_specs = (P("col", "row"), P("row", "col"), P("row", "col"), P("col", "row"), P("col", "row"))
    out_specs = (
        P("col", "row"),
        P("col", "row"),
        P("row", "col"),
        P("row", "col"),
        P("col", "row"),
    )
    return jax.shard_map(
        on_device, mesh=mesh, in_specs=in_specs, out_specs=out_specs, check_vma=False
    )
```

```python
import functools

import jax
import jax.numpy as jnp
from jax import lax
from jax.experimental import pallas as pl
from jax.experimental.pallas import tpu as pltpu
from jax.sharding import PartitionSpec as P


BF16, F32 = jnp.bfloat16, jnp.float32
SIDE = 4
DEEP = 8
BLOCKS = 16
VMEM_LIMIT = 24 * 1024 * 1024


def contract(left, right, left_dim, right_dim):
    return lax.dot_general(
        left, right, (((left_dim,), (right_dim,)), ((), ())), preferred_element_type=F32
    )


def shift(k, along):
    pairs = []
    for y in range(SIDE):
        for x in range(SIDE):
            for c in range(2 * DEEP):
                dy, dx = along if c % 2 == 0 else along[::-1]
                row = (y + k * dy) % SIDE * SIDE + (x + k * dx) % SIDE
                pairs.append(((y * SIDE + x) * 2 * DEEP + c, row * 2 * DEEP + c))
    return pairs


MAJOR, MINOR = (0, 1), (1, 0)


def partner():
    return [(c, c ^ 1) for c in range(2 * DEEP)]


def call(kernel, outs, args, n_scalar=0, scratch=(), keep=True):
    vmem = pl.BlockSpec(memory_space=pltpu.VMEM)
    smem = pl.BlockSpec(memory_space=pltpu.SMEM)
    make = pltpu.VMEM if keep else jax.ShapeDtypeStruct
    held = [pltpu.with_memory_space_constraint(a, pltpu.VMEM) for a in args[n_scalar:]]
    return pl.pallas_call(
        kernel,
        out_shape=[make(s, d) for s, d in outs],
        in_specs=[smem] * n_scalar + [vmem] * len(held),
        out_specs=[vmem] * len(outs),
        scratch_shapes=scratch,
        compiler_params=pltpu.CompilerParams(vmem_limit_bytes=VMEM_LIMIT),
    )(*args[:n_scalar], *held)


def take_blocks(order, source, target):
    rows = source.shape[0] // BLOCKS
    for s in range(BLOCKS):
        at = pl.ds(pl.multiple_of(order[s] * rows, rows), rows)
        target[s * rows : (s + 1) * rows] = source[at, :]


def partial_kernel(dim, order, left, *refs):
    *weights, keep, send1, send2, send3, mine = refs

    take_blocks(order, left, mine)
    group = keep.shape[1]
    for n, weight in enumerate(weights):
        value = contract(mine[...], weight[...], 1, dim)
        keep[n] = value[:group]
        for k, send in enumerate((send1, send2, send3)):
            send[n] = value[(k + 1) * group : (k + 2) * group].astype(BF16)


def first_sum_kernel(keep, got1, got2, got3, *outs):
    rows = outs[0].shape[1]
    for k, out in enumerate(outs):
        at = slice(k * rows, (k + 1) * rows)
        total = keep[:, at, :]
        for got in (got1, got2, got3):
            total = total + got[:, at, :].astype(F32)
        out[...] = total.astype(out.dtype)


def last_sum(n, own, *gots):
    return own[n] + sum(got[n].astype(F32) for got in gots)


def hidden_kernel(*refs):
    sums, (hidden, factors) = refs[:SIDE], refs[SIDE:]
    gate, up = last_sum(0, *sums), last_sum(1, *sums)
    sig = jax.nn.sigmoid(gate)
    hidden[0] = (gate * sig * up).astype(BF16)
    factors[0] = up * (sig * (1.0 + gate * (1.0 - sig)))
    factors[1] = gate * sig


def parts_kernel(factors, *refs):
    sums, (parts,) = refs[:SIDE], refs[SIDE:]
    grad = last_sum(0, *sums)
    for n in range(2):
        parts[n] = (grad * factors[n]).astype(BF16)


def join_kernel(*refs):
    blocks, (out,) = refs[:SIDE], refs[SIDE:]
    rows = blocks[0].shape[1]
    for k, block in enumerate(blocks):
        out[:, k * rows : (k + 1) * rows, :] = block[...]


def stack_rows(pieces, n, target):
    rows = pieces[0].shape[1]
    for k, piece in enumerate(pieces):
        target[k * rows : (k + 1) * rows] = piece[n]


def product_kernel(dim, place, *refs):
    pieces, weights = refs[:SIDE], refs[SIDE:-3]
    mine, theirs, stack = refs[-3:]
    rows = stack.shape[0] // BLOCKS
    value = None
    for n, weight in enumerate(weights):
        stack_rows(pieces, n, stack)
        term = contract(stack[...], weight[...], 1, dim)
        value = term if value is None else value + term
    for s in range(BLOCKS):
        to, block = place[s], value[s * rows : (s + 1) * rows]

        @pl.when(to < DEEP)
        def _():
            mine[pl.ds(pl.multiple_of(to * rows, rows), rows), :] = block

        @pl.when(to >= DEEP)
        def _():
            theirs[pl.ds(pl.multiple_of((to - DEEP) * rows, rows), rows), :] = block


def down_grad_kernel(order, og, *refs):
    pieces, (down_grad, mine, stack) = refs[:SIDE], refs[SIDE:]
    take_blocks(order, og, mine)
    stack_rows(pieces, 0, stack)
    down_grad[...] = contract(stack[...], mine[...], 0, 0).astype(BF16)


def weight_grads_kernel(order, x, *refs):
    pieces, (gate_grad, up_grad, mine, stack) = refs[:SIDE], refs[SIDE:]
    take_blocks(order, x, mine)
    for n, grad in enumerate((gate_grad, up_grad)):
        stack_rows(pieces, n, stack)
        grad[...] = contract(mine[...], stack[...], 0, 0).astype(BF16)


def send(value, k, along):
    return lax.ppermute(value, ("row", "col"), shift(k, along))


def spread(values, along):
    return [send(v, k + 1, along) for k, v in enumerate(values)]


def collect(value, along):
    return [value] + [send(value, -k, along) for k in range(1, SIDE)]


def z_reduce(mine, theirs, wire, same_core):
    total = (mine + lax.ppermute(theirs, "col", partner())).astype(wire)
    got = lax.all_to_all(total, "col", 0, 0, axis_index_groups=same_core, tiled=True)
    return jnp.sum(got.reshape(DEEP, -1, got.shape[1]).astype(F32), axis=0).astype(BF16)


def on_device(inputs, gate_weight, up_weight, down_weight, out_grad):
    deep, width = gate_weight.shape
    row, col = lax.axis_index("row"), lax.axis_index("col")
    y, x, core = row // SIDE, row % SIDE, col % 2
    slot = jnp.arange(BLOCKS, dtype=jnp.int32)
    outer, inner = slot // SIDE, slot % SIDE
    dy, dx = jnp.where(core == 0, inner, outer), jnp.where(core == 0, outer, inner)
    order = (y + dy) % SIDE * SIDE + (x + dx) % SIDE
    place = (order + core) % 2 * DEEP + order // 2
    same_core = [[2 * z + c for z in range(DEEP)] for c in range(2)]

    all_inputs = lax.all_gather(inputs, "col", axis=0, tiled=True)
    tokens = all_inputs.shape[0]
    rows = tokens // BLOCKS
    group = SIDE * rows

    def partials(left, weights, dim):
        n = len(weights)
        return call(
            functools.partial(partial_kernel, dim),
            [((n, group, width), F32)] + [((n, group, width), BF16)] * 3,
            (order, left, *weights),
            1,
            [pltpu.VMEM((tokens, deep), BF16)],
        )

    def product(pieces, weights, dim):
        return call(
            functools.partial(product_kernel, dim),
            [((tokens // 2, deep), F32)] * 2,
            (place, *pieces, *weights),
            1,
            [pltpu.VMEM((tokens, width), BF16)],
        )

    keep_gu, *sends = partials(all_inputs, (gate_weight, up_weight), 0)
    got_gu = spread(sends, MAJOR)
    out_grad, keep_gu = lax.optimization_barrier((out_grad, keep_gu))
    all_grads = lax.all_gather(out_grad, "col", axis=0, tiled=True)
    keep_h, *sends = partials(all_grads, (down_weight,), 1)
    got_h = spread(sends, MAJOR)

    def first_sum(keep, got):
        n = keep.shape[0]
        return call(
            first_sum_kernel,
            [((n, rows, width), F32)] + [((n, rows, width), BF16)] * 3,
            (keep, *got),
        )

    def join(blocks):
        n = blocks[0].shape[0]
        (out,) = call(join_kernel, [((n, group, width), BF16)], blocks)
        return out

    own_gu, *sends = first_sum(keep_gu, got_gu)
    got_gu = spread(sends, MINOR)
    own_h, *sends = first_sum(keep_h, got_h)
    got_h = spread(sends, MINOR)
    hidden, factors = call(
        hidden_kernel,
        [((1, rows, width), BF16), ((2, rows, width), F32)],
        (own_gu, *got_gu),
    )
    blocks_hidden = collect(hidden, MINOR)
    (parts,) = call(parts_kernel, [((2, rows, width), BF16)], (factors, own_h, *got_h))
    blocks_parts = collect(parts, MINOR)
    hiddens = collect(join(blocks_hidden), MAJOR)
    grads = collect(join(blocks_parts), MAJOR)

    scratch = [pltpu.VMEM((tokens, deep), BF16), pltpu.VMEM((tokens, width), BF16)]
    sums = product(hiddens, (down_weight,), 0)
    output = z_reduce(*sums, BF16, same_core)
    (down_grad,) = call(
        down_grad_kernel, [((width, deep), BF16)], (order, all_grads, *hiddens),
        1, scratch, keep=False,
    )
    sums = product(grads, (gate_weight, up_weight), 1)
    in_grad = z_reduce(*sums, BF16, same_core)
    gate_grad, up_grad = call(
        weight_grads_kernel, [((deep, width), BF16)] * 2, (order, all_inputs, *grads),
        1, scratch, keep=False,
    )
    return (output, in_grad, gate_grad, up_grad, down_grad)


def solution(mesh):
    in_specs = (P("col", "row"), P("row", "col"), P("row", "col"), P("col", "row"), P("col", "row"))
    out_specs = (
        P("col", "row"),
        P("col", "row"),
        P("row", "col"),
        P("row", "col"),
        P("col", "row"),
    )
    return jax.shard_map(
        on_device, mesh=mesh, in_specs=in_specs, out_specs=out_specs, check_vma=False
    )
```
